512 devices in a mesh: blk: 64 (over z, y_lo, core), head: 8 (over x, y_hi).
Axes of the slice: x: 4, y: 8 (y_hi: 2, y_lo: 4; y = y_hi * 4 + y_lo), z: 8, core: 2. Of those that a mesh axis runs over, the one named last changes fastest.
Arguments:
- queries: bfloat16 [4096, 3584], P('blk', 'head'), may hold values from -64 to 64
- new_keys: bfloat16 [4096, 3584], P('blk', 'head'), may hold values from -6 to 6
- new_values: bfloat16 [4096, 3584], P('blk', 'head'), may hold values from -6 to 6
- key_cache: bfloat16 [512, 128, 3584], P('blk', None, 'head'), may hold values from -6 to 6
- value_cache: bfloat16 [512, 128, 3584], P('blk', None, 'head'), may hold values from -6 to 6
- out_weight: bfloat16 [3584, 3584], P('head'), may hold values from -0.09375 to 0.09375
- cache_len: int32 [4], replicated, may hold values from 1 to 16384, as said below
- page_table: int32 [512], replicated, may hold values from 0 to 511, each once
- block_perm: int32 [64], replicated, may hold values from 0 to 63, each once
Outputs:
- projected: bfloat16 [4096, 3584], P('blk', 'head')
The draws below stay inside these ranges and needn't reach their ends.
Inputs may be any that keep to these rules, and one draw needn't show every extreme that they name: `cache_len`: some request has exactly 16384 cached tokens. `page_table`: each global page appears once. `block_perm`: each query block appears once.
All inputs are finite; a program needn't handle non-finite values.
Results may differ from the reference program's by a relative error of at most 0.015.
Values may be sent and summed in bfloat16 or wider, within the bound.
No kernel may reach another device: no remote copies, remote signals or barrier semaphores. Data moves between devices by JAX's collectives and lax.ppermute only.
A program may use at most 128 MiB of HBM per device.

```python
import math
import jax
import jax.numpy as jnp
from jax import lax

HEADS = 16
HD = 224
D_OUT = 3584
PAGE = 128
NEW = 1024
TOK_DEV = 64
TOKENS = 4096
REQS = 4
NPAGES = 512
LMAX = 16384
MAXP = 128
N_BLK = 64


def draw_queries(key, part):
    base_key = jax.random.fold_in(key, 1)
    drawn = jnp.clip(jax.random.normal(base_key, (TOKENS, HEADS * HD), jnp.float32), -6.0, 6.0)
    return drawn.astype(jnp.bfloat16)


def draw_key_cache(key, part):
    array_shape = (NPAGES, PAGE, HEADS * HD)
    base_key = jax.random.fold_in(key, 5)
    drawn = jnp.clip(jax.random.normal(base_key, array_shape, jnp.float32), -6.0, 6.0)
    return drawn.astype(jnp.bfloat16)


def draw_cache_len(key, part):
    lengths = jax.random.randint(jax.random.fold_in(key, 3), (REQS,), 1, LMAX + 1)
    longest = jax.random.randint(jax.random.fold_in(key, 4), (), 0, REQS)
    return jnp.where(jnp.arange(REQS) == longest, LMAX, lengths).astype(jnp.int32)


def block_levels(stream_key, shape, split, smallest, largest):
    gain, own = 1.0, jax.random.fold_in(stream_key, 6)
    for position, blocks in split:
        draws = jnp.exp(jax.random.uniform(jax.random.fold_in(own, position), (blocks,), jnp.float32, smallest / len(split), largest / len(split)))
        gain = gain * jnp.repeat(draws, shape[position] // blocks).reshape([-1 if axis == position else 1 for axis in range(len(shape))])
    return gain


def bell_draw(own_key, shape, spread, bound, cuts=(), kind=jnp.bfloat16):
    values = jax.random.normal(own_key, shape, jnp.float32) * spread
    if len(cuts) > 0:
        values = block_levels(own_key, shape, cuts, -0.22, 0.18) * values
    return jnp.clip(values, min=-bound, max=bound).astype(kind)


def setup_inputs(seed: int = 0) -> dict:
    streams_of = jax.random.split(jax.random.key(seed), 10)
    return {
        "queries": draw_queries(jax.random.fold_in(streams_of[9], 71), 0),
        "new_keys": bell_draw(streams_of[1], (TOKENS, HEADS * HD), 1.0, 6.0, ((0, 64), (1, 8))),
        "new_values": bell_draw(streams_of[2], (TOKENS, HEADS * HD), 1.0, 6.0, ((0, 64), (1, 8))),
        "key_cache": draw_key_cache(jax.random.fold_in(streams_of[9], 71), 0),
        "value_cache": bell_draw(streams_of[4], (NPAGES, PAGE, HEADS * HD), 1.0, 6.0, ((0, 64), (2, 8))),
        "out_weight": bell_draw(streams_of[5], (HEADS * HD, D_OUT), (HEADS * HD) ** -0.5, 0.09375, ((0, 8),)),
        "cache_len": draw_cache_len(jax.random.fold_in(streams_of[9], 71), 0),
        "page_table": jax.random.permutation(streams_of[7], NPAGES).astype(jnp.int32),
        "block_perm": jax.random.permutation(streams_of[8], N_BLK).astype(jnp.int32),
    }


def reference(queries, new_keys, new_values, key_cache, value_cache, out_weight, cache_len, page_table, block_perm):
    row_width = HEADS * HD
    block_ids = jnp.arange(N_BLK, dtype=jnp.int32)
    inverse = jnp.zeros((N_BLK,), jnp.int32).at[block_perm].set(block_ids)

    def to_global(dealt):
        return dealt.reshape(N_BLK, TOK_DEV, row_width)[inverse].reshape(REQS, NEW, row_width)
    query_all = to_global(queries)
    key_new = to_global(new_keys)
    value_new = to_global(new_values)
    page_grid = page_table.reshape(REQS, MAXP)
    score_scale = 1.0 / math.sqrt(HD)

    def one_request(request):
        page_rows = page_grid[request]
        key_rows = jnp.concatenate([key_cache[page_rows].reshape(LMAX, row_width), key_new[request]], axis=0)
        value_rows = jnp.concatenate([value_cache[page_rows].reshape(LMAX, row_width), value_new[request]], axis=0)
        positions = jnp.arange(LMAX + NEW, dtype=jnp.int32)[None, :]
        new_pos = jnp.arange(NEW, dtype=jnp.int32)[:, None]
        visible = jnp.where(positions < LMAX, positions < cache_len[request], positions - LMAX <= new_pos)
        query_rows = query_all[request]

        def one_head(head_index):
            start = head_index * HD
            q_part = lax.dynamic_slice_in_dim(query_rows, start, HD, 1)
            k_part = lax.dynamic_slice_in_dim(key_rows, start, HD, 1)
            v_part = lax.dynamic_slice_in_dim(value_rows, start, HD, 1)
            scores = jnp.dot(q_part, k_part.T, preferred_element_type=jnp.float32) * score_scale
            scores = jnp.where(visible, scores, -1e+30)
            row_top = lax.optimization_barrier(jnp.max(scores, axis=1, keepdims=True))
            weights = jnp.where(visible, jnp.exp(scores - row_top), 0.0)
            rounded = lax.optimization_barrier(weights.astype(jnp.bfloat16))
            total = lax.optimization_barrier(jnp.sum(rounded.astype(jnp.float32), axis=1, keepdims=True))
            numer = jnp.dot(rounded, v_part, preferred_element_type=jnp.float32)
            return numer / total
        head_outs = lax.map(one_head, jnp.arange(HEADS, dtype=jnp.int32))
        return jnp.transpose(head_outs, (1, 0, 2)).reshape(NEW, row_width)
    attended = lax.map(one_request, jnp.arange(REQS, dtype=jnp.int32))
    dealt = attended.reshape(N_BLK, TOK_DEV, row_width)[block_perm].reshape(N_BLK * TOK_DEV, row_width)
    mixed = dealt.astype(jnp.bfloat16)
    return jnp.dot(mixed, out_weight, preferred_element_type=jnp.float32).astype(jnp.bfloat16)
```

```python
import functools
import math

import jax
import jax.numpy as jnp
from jax import lax
from jax.experimental import pallas as pl
from jax.experimental.pallas import tpu as pltpu
from jax.sharding import PartitionSpec as P

HD = 224
PAGE = 128
P_DEV = 8
NEW = 1024
TOK_DEV = 64
MAXP = 128
REQS = 4
N_BLK = 64
BLK_PER_REQ = NEW // TOK_DEV
WIDE = 256
TQ = 512
QB = TQ // TOK_DEV
SLOTS = 2 * P_DEV + 2
POS = 24
LOG2_SCALE = math.log2(math.e) / math.sqrt(HD)
FLOOR = -1e20
MASKED = -1e30
K_ROWS = P_DEV * PAGE
PACK = 2 * K_ROWS + 2 * TOK_DEV


def attend(req, fill, off, inv, q_ref, own_ref, other_ref, out_ref, k_s, v_s, acc, top, pfill, poff, ends):
    lane = lax.broadcasted_iota(jnp.int32, (POS * PAGE, WIDE), 1)
    v_s[...] = jnp.where(lane >= HD, 1.0, 0.0).astype(jnp.bfloat16)
    for p in range(POS):
        pfill[p] = 0
        poff[p] = 0
    place = [jnp.int32(POS - 2)] * SLOTS
    pos = jnp.int32(0)
    for r in range(REQS):
        ends[2 * r] = pos // 2
        for i in range(SLOTS):
            hit = jnp.logical_and(req[i] == r, fill[i] > 0)
            place[i] = jnp.where(hit, pos, place[i])
            pos = pos + jnp.where(hit, 1, 0)
        pos = (pos + 1) // 2 * 2
        ends[2 * r + 1] = pos // 2
    for i in range(SLOTS):
        pfill[place[i]] = fill[i]
        poff[place[i]] = off[i]
        if i < 2 * P_DEV:
            src = own_ref if i < P_DEV else other_ref
            row = (i % P_DEV) * PAGE
            dst = pl.ds(pl.multiple_of(place[i] * PAGE, PAGE), PAGE)
            k_s[dst, :] = src[row : row + PAGE, :]
            v_s[dst, :HD] = src[K_ROWS + row : K_ROWS + row + PAGE, :]
        else:
            src = own_ref if i == 2 * P_DEV else other_ref
            row = 2 * K_ROWS
            dst = pl.ds(pl.multiple_of(place[i] * PAGE, PAGE), TOK_DEV)
            k_s[dst, :] = src[row : row + TOK_DEV, :]
            v_s[dst, :HD] = src[row + TOK_DEV : row + 2 * TOK_DEV, :]

    key_id = lax.broadcasted_iota(jnp.int32, (TQ, PAGE), 1)
    row_id = lax.broadcasted_iota(jnp.int32, (TQ, PAGE), 0)
    out_lane = lax.broadcasted_iota(jnp.int32, (TQ, WIDE), 1)

    def tile(step, _):
        r = step // (NEW // TQ)
        t = step % (NEW // TQ)
        first = step * QB
        q = jnp.concatenate([q_ref[inv[first + u]] for u in range(QB)], axis=0)
        acc[...] = jnp.zeros((TQ, WIDE), jnp.float32)
        top[...] = jnp.full((TQ, PAGE), FLOOR, jnp.float32)
        row_pos = row_id + t * TQ

        def chunk(c, _):
            at = pl.ds(pl.multiple_of(c * 2 * PAGE, 2 * PAGE), 2 * PAGE)
            s = lax.dot_general(q, k_s[at, :], (((1,), (1,)), ((), ())), preferred_element_type=jnp.float32)
            parts = []
            for half in range(2):
                limit = jnp.minimum(row_pos - poff[2 * c + half], pfill[2 * c + half] - 1)
                s_half = s[:, half * PAGE : (half + 1) * PAGE] * LOG2_SCALE
                parts.append(jnp.where(key_id <= limit, s_half, MASKED))
            old = top[...]
            best = jnp.max(jnp.maximum(parts[0], parts[1]), axis=1, keepdims=True)
            new = jnp.maximum(old, best)
            w = jnp.concatenate([jnp.exp2(x - new).astype(jnp.bfloat16) for x in parts], axis=1)
            factor = jnp.exp2(old - new)
            part = jnp.dot(w, v_s[at, :], preferred_element_type=jnp.float32)
            acc[:, :PAGE] = acc[:, :PAGE] * factor + part[:, :PAGE]
            acc[:, PAGE:] = acc[:, PAGE:] * factor + part[:, PAGE:]
            top[...] = new
            return 0

        lax.fori_loop(ends[2 * r], ends[2 * r + 1], chunk, 0)
        old = top[...]
        up = old + jnp.abs(old) * (2.0**-15)
        high = up.astype(jnp.bfloat16).astype(jnp.float32)
        low = (up - high).astype(jnp.bfloat16).astype(jnp.float32)
        factor = jnp.exp2(old - (high + low))
        left = acc[:, :PAGE] * factor
        right = acc[:, PAGE:] * factor
        total = jnp.broadcast_to(right[:, HD - PAGE : HD - PAGE + 1], (TQ, PAGE))
        total_low = total - total.astype(jnp.bfloat16).astype(jnp.float32)
        tail = key_id + PAGE
        right = jnp.where(tail == HD + 1, high, right)
        right = jnp.where(tail == HD + 2, low, right)
        right = jnp.where(tail == HD + 3, total_low, right)
        result = jnp.concatenate([left.astype(jnp.bfloat16), right.astype(jnp.bfloat16)], axis=1)
        for u in range(QB):
            out_ref[inv[first + u]] = result[u * TOK_DEV : (u + 1) * TOK_DEV]
        return 0

    lax.fori_loop(0, REQS * NEW // TQ, tile, 0)


def merge_project(x_ref, w_ref, out_ref, mixed):
    n_src = N_BLK // 2
    for h in range(2):

        def top_of(s, best):
            x = x_ref[2 * s + h, :, PAGE:].astype(jnp.float32)
            return jnp.maximum(best, x[:, HD + 1 - PAGE : HD + 2 - PAGE] + x[:, HD + 2 - PAGE : HD + 3 - PAGE])

        best = lax.fori_loop(0, n_src, top_of, jnp.full((TOK_DEV, 1), MASKED, jnp.float32), unroll=4)

        def add(s, total):
            x = x_ref[2 * s + h].astype(jnp.float32)
            here = x[:, HD + 1 : HD + 2] + x[:, HD + 2 : HD + 3]
            return total + x * jnp.exp2(here - best)

        total = lax.fori_loop(0, n_src, add, jnp.zeros((TOK_DEV, WIDE), jnp.float32), unroll=4)
        mass = total[:, HD : HD + 1] + total[:, HD + 3 : HD + 4]
        mixed[:, h * HD : (h + 1) * HD] = (total[:, :HD] / mass).astype(jnp.bfloat16)
    y = jnp.dot(mixed[...], w_ref[...], preferred_element_type=jnp.float32)
    width = out_ref.shape[2]
    for h in range(out_ref.shape[0]):
        out_ref[h] = y[:, h * width : (h + 1) * width].astype(jnp.bfloat16)


def shards(queries, new_keys, new_values, key_cache, value_cache, out_weight, cache_len, page_table, block_perm):
    row_width = queries.shape[1]
    me = lax.axis_index("blk")
    core = me % 2
    partner = me + 1 - 2 * core

    def half(x, which):
        return jnp.where(which == 0, x[:, :HD], x[:, HD:])

    packed = jnp.concatenate(
        [key_cache.reshape(K_ROWS, row_width), value_cache.reshape(K_ROWS, row_width), new_keys, new_values], axis=0
    )
    own = half(packed, core)
    send = half(packed, 1 - core)
    other = lax.ppermute(send, "blk", [(d, d ^ 1) for d in range(N_BLK)])

    spread = jnp.broadcast_to(
        jnp.stack([queries[:, :HD], queries[:, HD:]])[None], (N_BLK // 2, 2, TOK_DEV, HD)
    ).reshape(N_BLK, TOK_DEV, HD)
    query_all = lax.all_to_all(spread, "blk", split_axis=0, concat_axis=0, tiled=True)

    page_ids = jnp.concatenate([me * P_DEV + jnp.arange(P_DEV), partner * P_DEV + jnp.arange(P_DEV)])
    table_ids = jnp.arange(page_table.shape[0], dtype=jnp.int32)
    logical = jnp.sum(jnp.where(page_table[None, :] == page_ids[:, None], table_ids[None, :], 0), axis=1)
    page_req = logical // MAXP
    req_ids = jnp.arange(REQS, dtype=jnp.int32)
    page_len = jnp.sum(jnp.where(page_req[:, None] == req_ids[None, :], cache_len[None, :], 0), axis=1)
    page_fill = jnp.clip(page_len - logical % MAXP * PAGE, 0, PAGE)
    block_ids = jnp.arange(N_BLK, dtype=jnp.int32)
    mine = jnp.stack([me, partner])
    new_block = jnp.sum(jnp.where(block_ids[None, :] == mine[:, None], block_perm[None, :], 0), axis=1)
    inverse = jnp.sum(jnp.where(block_perm[None, :] == block_ids[:, None], block_ids[None, :], 0), axis=1)
    req = jnp.concatenate([page_req, new_block // BLK_PER_REQ]).astype(jnp.int32)
    fill = jnp.concatenate([page_fill, jnp.full((2,), TOK_DEV, jnp.int32)]).astype(jnp.int32)
    off = jnp.concatenate(
        [jnp.full((2 * P_DEV,), -(2**20), jnp.int32), new_block % BLK_PER_REQ * TOK_DEV]
    ).astype(jnp.int32)

    whole = pl.BlockSpec(memory_space=pltpu.VMEM)
    partial = pl.pallas_call(
        attend,
        out_shape=jax.ShapeDtypeStruct((N_BLK, TOK_DEV, WIDE), jnp.bfloat16),
        in_specs=[pl.BlockSpec(memory_space=pltpu.SMEM)] * 4 + [whole] * 3,
        out_specs=whole,
        scratch_shapes=[
            pltpu.VMEM((POS * PAGE, HD), jnp.bfloat16),
            pltpu.VMEM((POS * PAGE, WIDE), jnp.bfloat16),
            pltpu.VMEM((TQ, WIDE), jnp.float32),
            pltpu.VMEM((TQ, PAGE), jnp.float32),
            pltpu.SMEM((POS,), jnp.int32),
            pltpu.SMEM((POS,), jnp.int32),
            pltpu.SMEM((2 * REQS,), jnp.int32),
        ],
        name="attend",
    )(req, fill, off, inverse.astype(jnp.int32), query_all, own, other)

    gathered = lax.all_to_all(partial, "blk", split_axis=0, concat_axis=0, tiled=True)
    n_head = lax.axis_size("head")
    terms = pl.pallas_call(
        merge_project,
        out_shape=jax.ShapeDtypeStruct((n_head, TOK_DEV, row_width), jnp.bfloat16),
        in_specs=[whole, whole],
        out_specs=whole,
        scratch_shapes=[pltpu.VMEM((TOK_DEV, row_width), jnp.bfloat16)],
        name="merge_project",
    )(gathered, out_weight)
    terms = lax.all_to_all(terms, "head", split_axis=0, concat_axis=0, tiled=True)
    return jnp.sum(terms.astype(jnp.float32), axis=0).astype(jnp.bfloat16)


def solution(mesh):
    in_specs = (
        P("blk", "head"),
        P("blk", "head"),
        P("blk", "head"),
        P("blk", None, "head"),
        P("blk", None, "head"),
        P("head", None),
        P(),
        P(),
        P(),
    )
    return jax.shard_map(shards, mesh=mesh, in_specs=in_specs, out_specs=P("blk", "head"), check_vma=False)
```

```python
import functools
import math

import jax
import jax.numpy as jnp
from jax import lax
from jax.experimental import pallas as pl
from jax.experimental.pallas import tpu as pltpu
from jax.sharding import PartitionSpec as P

HD = 224
PAGE = 128
P_DEV = 8
NEW = 1024
TOK_DEV = 64
MAXP = 128
REQS = 4
N_BLK = 64
BLK_PER_REQ = NEW // TOK_DEV
WIDE = 256
TQ = 512
QB = TQ // TOK_DEV
SLOTS = 2 * P_DEV + 2
POS = 24
LOG2_SCALE = math.log2(math.e) / math.sqrt(HD)
FLOOR = -1e20
MASKED = -1e30
LIMIT = 40 << 20
K_ROWS = P_DEV * PAGE
CHIPS = N_BLK // 2
CHIP_ROWS = 2 * TOK_DEV
TAIL = HD - PAGE
STEP = PAGE - TAIL
Q_PACK = CHIP_ROWS * HD // PAGE
PACK = 2 * K_ROWS + 2 * TOK_DEV


def attend(req, fill, off, inv, q_ref, own_ref, other_ref, out_ref, k_s, v_s, q_s, acc, top, pfill, poff, ends):
    lane = lax.broadcasted_iota(jnp.int32, (POS * PAGE, WIDE), 1)
    v_s[...] = jnp.where(lane >= HD, 1.0, 0.0).astype(jnp.bfloat16)
    for p in range(POS):
        pfill[p] = 0
        poff[p] = 0
    place = [jnp.int32(POS - 2)] * SLOTS
    pos = jnp.int32(0)
    for r in range(REQS):
        ends[2 * r] = pos // 2
        for i in range(SLOTS):
            hit = jnp.logical_and(req[i] == r, fill[i] > 0)
            place[i] = jnp.where(hit, pos, place[i])
            pos = pos + jnp.where(hit, 1, 0)
        pos = (pos + 1) // 2 * 2
        ends[2 * r + 1] = pos // 2
    for i in range(SLOTS):
        pfill[place[i]] = fill[i]
        poff[place[i]] = off[i]
        if i < 2 * P_DEV:
            src = own_ref if i < P_DEV else other_ref
            row = (i % P_DEV) * PAGE
            dst = pl.ds(pl.multiple_of(place[i] * PAGE, PAGE), PAGE)
            k_s[dst, :] = src[row : row + PAGE, :]
            v_s[dst, :HD] = src[K_ROWS + row : K_ROWS + row + PAGE, :]
        else:
            src = own_ref if i == 2 * P_DEV else other_ref
            row = 2 * K_ROWS
            dst = pl.ds(pl.multiple_of(place[i] * PAGE, PAGE), TOK_DEV)
            k_s[dst, :] = src[row : row + TOK_DEV, :]
            v_s[dst, :HD] = src[row + TOK_DEV : row + 2 * TOK_DEV, :]

    def unfold(i, _):
        for b in range(2):
            q_s[2 * i + b, :, :PAGE] = q_ref[i, b * TOK_DEV : (b + 1) * TOK_DEV, :]
        q_s[2 * i, :, PAGE:] = q_ref[i, PAGE : PAGE + TOK_DEV, :TAIL]
        q_s[2 * i + 1, :STEP, PAGE:] = q_ref[i, PAGE + TOK_DEV : PAGE + TAIL, :TAIL]
        q_s[2 * i + 1, STEP:, PAGE:] = jnp.concatenate(
            [q_ref[i, PAGE + k * STEP : PAGE + (k + 1) * STEP, TAIL:] for k in range(TAIL // STEP)], axis=1
        )
        return 0

    lax.fori_loop(0, CHIPS, unfold, 0, unroll=2)

    key_id = lax.broadcasted_iota(jnp.int32, (TQ, PAGE), 1)
    row_id = lax.broadcasted_iota(jnp.int32, (TQ, PAGE), 0)
    out_lane = lax.broadcasted_iota(jnp.int32, (TQ, WIDE), 1)

    def tile(step, _):
        r = step // (NEW // TQ)
        t = step % (NEW // TQ)
        first = step * QB
        q = jnp.concatenate([q_s[inv[first + u]] for u in range(QB)], axis=0)
        acc[...] = jnp.zeros((TQ, WIDE), jnp.float32)
        top[...] = jnp.full((TQ, PAGE), FLOOR, jnp.float32)
        row_pos = row_id + t * TQ

        def chunk(c, _):
            at = pl.ds(pl.multiple_of(c * 2 * PAGE, 2 * PAGE), 2 * PAGE)
            s = lax.dot_general(q, k_s[at, :], (((1,), (1,)), ((), ())), preferred_element_type=jnp.float32)
            parts = []
            for half in range(2):
                limit = jnp.minimum(row_pos - poff[2 * c + half], pfill[2 * c + half] - 1)
                s_half = s[:, half * PAGE : (half + 1) * PAGE] * LOG2_SCALE
                parts.append(jnp.where(key_id <= limit, s_half, MASKED))
            old = top[...]
            best = jnp.max(jnp.maximum(parts[0], parts[1]), axis=1, keepdims=True)
            new = jnp.maximum(old, best)
            w = jnp.concatenate([jnp.exp2(x - new).astype(jnp.bfloat16) for x in parts], axis=1)
            factor = jnp.exp2(old - new)
            part = jnp.dot(w, v_s[at, :], preferred_element_type=jnp.float32)
            acc[:, :PAGE] = acc[:, :PAGE] * factor + part[:, :PAGE]
            acc[:, PAGE:] = acc[:, PAGE:] * factor + part[:, PAGE:]
            top[...] = new
            return 0

        lax.fori_loop(ends[2 * r], ends[2 * r + 1], chunk, 0)
        old = top[...]
        up = old + jnp.abs(old) * (2.0**-15)
        high = up.astype(jnp.bfloat16).astype(jnp.float32)
        low = (up - high).astype(jnp.bfloat16).astype(jnp.float32)
        factor = jnp.exp2(old - (high + low))
        left = acc[:, :PAGE] * factor
        right = acc[:, PAGE:] * factor
        total = jnp.broadcast_to(right[:, HD - PAGE : HD - PAGE + 1], (TQ, PAGE))
        total_low = total - total.astype(jnp.bfloat16).astype(jnp.float32)
        tail = key_id + PAGE
        right = jnp.where(tail == HD + 1, high, right)
        right = jnp.where(tail == HD + 2, low, right)
        right = jnp.where(tail == HD + 3, total_low, right)
        result = jnp.concatenate([left.astype(jnp.bfloat16), right.astype(jnp.bfloat16)], axis=1)
        for u in range(QB):
            out_ref[inv[first + u]] = result[u * TOK_DEV : (u + 1) * TOK_DEV]
        return 0

    lax.fori_loop(0, REQS * NEW // TQ, tile, 0)


def fold_queries(core, own_ref, other_ref, out_ref, chip):
    mine = pl.ds(pl.multiple_of(core[0] * TOK_DEV, TOK_DEV), TOK_DEV)
    theirs = pl.ds(pl.multiple_of((1 - core[0]) * TOK_DEV, TOK_DEV), TOK_DEV)
    chip[mine, :] = own_ref[...]
    chip[theirs, :] = other_ref[...]
    rows = chip[...]
    tail = rows[:, PAGE:]
    folded = jnp.concatenate([tail[TAIL:, k * STEP : (k + 1) * STEP] for k in range(TAIL // STEP)], axis=0)
    pack = jnp.concatenate([rows[:, :PAGE], jnp.concatenate([tail[:TAIL], folded], axis=1)], axis=0)
    out_ref[...] = jnp.broadcast_to(pack[None], (CHIPS, Q_PACK, PAGE))


def merge(core, x_ref, mine_ref, theirs_ref, tops, acc, rows):
    def top_of(s, best):
        x = x_ref[s, :, PAGE:].astype(jnp.float32)
        here = x[:, TAIL + 1 : TAIL + 2] + x[:, TAIL + 2 : TAIL + 3]
        here = jnp.broadcast_to(here, (CHIP_ROWS, PAGE))
        tops[s] = here
        return jnp.maximum(best, here)

    best = lax.fori_loop(0, CHIPS, top_of, jnp.full((CHIP_ROWS, PAGE), MASKED, jnp.float32), unroll=4)
    acc[...] = jnp.zeros((CHIP_ROWS, WIDE), jnp.float32)

    def add(g, _):
        for part in range(2):
            lanes = slice(part * PAGE, (part + 1) * PAGE)
            total = acc[:, lanes]
            for u in range(4):
                factor = jnp.exp2(tops[4 * g + u] - best)
                total = total + x_ref[4 * g + u, :, lanes].astype(jnp.float32) * factor
            acc[:, lanes] = total
        return 0

    lax.fori_loop(0, CHIPS // 4, add, 0)
    total = acc[...]
    mass = total[:, HD : HD + 1] + total[:, HD + 3 : HD + 4]
    rows[...] = (total[:, :HD] / mass).astype(jnp.bfloat16)
    mine_ref[...] = rows[pl.ds(pl.multiple_of(core[0] * TOK_DEV, TOK_DEV), TOK_DEV), :]
    theirs_ref[...] = rows[pl.ds(pl.multiple_of((1 - core[0]) * TOK_DEV, TOK_DEV), TOK_DEV), :]


def project(core, mine_ref, other_ref, w_ref, out_ref):
    mine_rows = pl.ds(pl.multiple_of(core[0] * HD, HD), HD)
    other_rows = pl.ds(pl.multiple_of((1 - core[0]) * HD, HD), HD)
    y = jnp.dot(mine_ref[...], w_ref[mine_rows, :], preferred_element_type=jnp.float32)
    y = y + jnp.dot(other_ref[...], w_ref[other_rows, :], preferred_element_type=jnp.float32)
    width = out_ref.shape[2]
    for h in range(out_ref.shape[0]):
        out_ref[h] = y[:, h * width : (h + 1) * width].astype(jnp.bfloat16)


def in_vmem(x):
    return pltpu.with_memory_space_constraint(x, pltpu.VMEM)


def shards(queries, new_keys, new_values, key_cache, value_cache, out_weight, cache_len, page_table, block_perm):
    row_width = queries.shape[1]
    me = lax.axis_index("blk")
    core = me % 2
    partner = me + 1 - 2 * core

    def half(x, which):
        return jnp.where(which == 0, x[:, :HD], x[:, HD:])

    packed = jnp.concatenate(
        [key_cache.reshape(K_ROWS, row_width), value_cache.reshape(K_ROWS, row_width), new_keys, new_values], axis=0
    )
    own = half(packed, core)
    send = half(packed, 1 - core)
    other = lax.ppermute(send, "blk", [(d, d ^ 1) for d in range(N_BLK)])

    swap = [(d, d ^ 1) for d in range(N_BLK)]
    groups = [[2 * i + c for i in range(CHIPS)] for c in range(2)]
    q_own = half(queries, core)
    q_other = lax.ppermute(half(queries, 1 - core), "blk", swap)
    whole = pl.BlockSpec(memory_space=pltpu.VMEM)
    scalar = pl.BlockSpec(memory_space=pltpu.SMEM)
    core_id = core.reshape(1).astype(jnp.int32)
    spread = pl.pallas_call(
        fold_queries,
        out_shape=pltpu.VMEM((CHIPS, Q_PACK, PAGE), jnp.bfloat16),
        in_specs=[scalar, whole, whole],
        out_specs=whole,
        scratch_shapes=[pltpu.VMEM((CHIP_ROWS, HD), jnp.bfloat16)],
        compiler_params=pltpu.CompilerParams(vmem_limit_bytes=LIMIT),
        name="fold_queries",
    )(core_id, q_own, q_other)
    query_all = lax.all_to_all(
        spread, "blk", split_axis=0, concat_axis=0, tiled=True, axis_index_groups=groups
    )

    page_ids = jnp.concatenate([me * P_DEV + jnp.arange(P_DEV), partner * P_DEV + jnp.arange(P_DEV)])
    table_ids = jnp.arange(page_table.shape[0], dtype=jnp.int32)
    logical = jnp.sum(jnp.where(page_table[None, :] == page_ids[:, None], table_ids[None, :], 0), axis=1)
    page_req = logical // MAXP
    req_ids = jnp.arange(REQS, dtype=jnp.int32)
    page_len = jnp.sum(jnp.where(page_req[:, None] == req_ids[None, :], cache_len[None, :], 0), axis=1)
    page_fill = jnp.clip(page_len - logical % MAXP * PAGE, 0, PAGE)
    block_ids = jnp.arange(N_BLK, dtype=jnp.int32)
    mine = jnp.stack([me, partner])
    new_block = jnp.sum(jnp.where(block_ids[None, :] == mine[:, None], block_perm[None, :], 0), axis=1)
    inverse = jnp.sum(jnp.where(block_perm[None, :] == block_ids[:, None], block_ids[None, :], 0), axis=1)
    req = jnp.concatenate([page_req, new_block // BLK_PER_REQ]).astype(jnp.int32)
    fill = jnp.concatenate([page_fill, jnp.full((2,), TOK_DEV, jnp.int32)]).astype(jnp.int32)
    off = jnp.concatenate(
        [jnp.full((2 * P_DEV,), -(2**20), jnp.int32), new_block % BLK_PER_REQ * TOK_DEV]
    ).astype(jnp.int32)

    partial = pl.pallas_call(
        attend,
        out_shape=pltpu.VMEM((N_BLK, TOK_DEV, WIDE), jnp.bfloat16),
        in_specs=[pl.BlockSpec(memory_space=pltpu.SMEM)] * 4 + [whole] * 3,
        out_specs=whole,
        scratch_shapes=[
            pltpu.VMEM((POS * PAGE, HD), jnp.bfloat16),
            pltpu.VMEM((POS * PAGE, WIDE), jnp.bfloat16),
            pltpu.VMEM((N_BLK, TOK_DEV, HD), jnp.bfloat16),
            pltpu.VMEM((TQ, WIDE), jnp.float32),
            pltpu.VMEM((TQ, PAGE), jnp.float32),
            pltpu.SMEM((POS,), jnp.int32),
            pltpu.SMEM((POS,), jnp.int32),
            pltpu.SMEM((2 * REQS,), jnp.int32),
        ],
        compiler_params=pltpu.CompilerParams(vmem_limit_bytes=LIMIT),
        name="attend",
    )(req, fill, off, inverse.astype(jnp.int32), in_vmem(query_all), own, other)

    gathered = lax.all_to_all(
        partial.reshape(CHIPS, CHIP_ROWS, WIDE),
        "blk",
        split_axis=0,
        concat_axis=0,
        tiled=True,
        axis_index_groups=groups,
    )
    n_head = lax.axis_size("head")
    mine_rows, their_rows = pl.pallas_call(
        merge,
        out_shape=[jax.ShapeDtypeStruct((TOK_DEV, HD), jnp.bfloat16)] * 2,
        in_specs=[scalar, whole],
        out_specs=[whole, whole],
        scratch_shapes=[
            pltpu.VMEM((CHIPS, CHIP_ROWS, PAGE), jnp.float32),
            pltpu.VMEM((CHIP_ROWS, WIDE), jnp.float32),
            pltpu.VMEM((CHIP_ROWS, HD), jnp.bfloat16),
        ],
        compiler_params=pltpu.CompilerParams(vmem_limit_bytes=LIMIT),
        name="merge",
    )(core_id, in_vmem(gathered))
    other_rows = lax.ppermute(their_rows, "blk", swap)
    terms = pl.pallas_call(
        project,
        out_shape=pltpu.VMEM((n_head, TOK_DEV, row_width), jnp.bfloat16),
        in_specs=[scalar, whole, whole, whole],
        out_specs=whole,
        compiler_params=pltpu.CompilerParams(vmem_limit_bytes=LIMIT),
        name="project",
    )(core_id, mine_rows, other_rows, out_weight)
    terms = lax.all_to_all(terms, "head", split_axis=0, concat_axis=0, tiled=True)
    return jnp.sum(terms.astype(jnp.float32), axis=0).astype(jnp.bfloat16)


def solution(mesh):
    in_specs = (
        P("blk", "head"),
        P("blk", "head"),
        P("blk", "head"),
        P("blk", None, "head"),
        P("blk", None, "head"),
        P("head", None),
        P(),
        P(),
        P(),
    )
    return jax.shard_map(shards, mesh=mesh, in_specs=in_specs, out_specs=P("blk", "head"), check_vma=False)
```
